256 devices in a mesh: seq: 32 (over y, x, core), grp: 8 (over z).
Axes of the slice: x: 4, y: 4, z: 8, core: 2. Of those that a mesh axis runs over, the one named last changes fastest.
Arguments:
- hidden_in: bfloat16 [98304, 2048], P(('grp', 'seq')), parts along dimension 0, may hold values from -8 to 8
- norm_gain: bfloat16 [2048], replicated, may hold values from 0.099609375 to 1.8984375
- w_query: bfloat16 [2048, 2048], P('seq'), may hold values from -1 to 1
- w_key: bfloat16 [2048, 128], P('seq'), may hold values from -1 to 1
- w_value: bfloat16 [2048, 128], P('seq'), may hold values from -0.125 to 0.125
- w_out: bfloat16 [2048, 2048], P('seq'), may hold values from -0.625 to 0.625
- seg_ids: int32 [98304], P('grp'), parts along dimension 0, may hold values from 0 to 1, never falling along the last dimension, each value on 1 to 11904 neighbouring positions
- cache_slot: int32 [768], P('grp'), parts along dimension 0, may hold values from 0 to 95, each once
Outputs:
- hidden_out: bfloat16 [98304, 2048], P(('grp', 'seq')), parts along dimension 0
- kv_cache: bfloat16 [98304, 256], P(('grp', 'seq')), parts along dimension 0
The draws below stay inside these ranges and needn't reach their ends.
There are 8 independent parts, one for each index of `grp`. The reference program is written for one: setup_inputs(seed, part) draws one part's arguments, and reference() takes and returns one part's arrays. A program takes and returns all parts, laid end to end along the dimension named above; an argument that names none is the same for every part. Nothing has to cross between parts.
Inputs may be any that keep to these rules, and one draw needn't show every extreme that they name: `seg_ids`: segment numbers never fall along the stream; each prompt holds 1 to 11904 tokens. `cache_slot`: every cache position appears exactly once.
All inputs are finite; a program needn't handle non-finite values.
Results may differ from the reference program's by a relative error of at most 0.01.
Values may be sent and summed in bfloat16 or wider, within the bound.
No kernel may reach another device: no remote copies, remote signals or barrier semaphores. Data moves between devices by JAX's collectives and lax.ppermute only.
A program may use at most 256 MiB of HBM per device.

```python
import math
import jax
import jax.numpy as jnp
import numpy as np
from jax import lax

D = 2048
HEADS = 16
HD = 128
WINDOW = 1024
CACHE_BLK = 128
TOK_DEV = 384
REACH = 3
TOKENS = 12288
SEGS = 2
BLOCKS = 96


def key_base(key):
    return jax.random.normal(jax.random.fold_in(key, 7), (D, HD), jnp.float32) / math.sqrt(D)


def draw_w_key(key, part):
    base = key_base(key)
    return jnp.clip(base, -1.0, 1.0).astype(jnp.bfloat16)


def draw_w_query(key, part):
    noise = jax.random.normal(jax.random.fold_in(key, 11), (D, HEADS, HD), jnp.float32) / math.sqrt(D)
    mixed = noise
    return jnp.clip(mixed.reshape(D, HEADS * HD), -1.0, 1.0).astype(jnp.bfloat16)


def draw_hidden_in(key, part):
    row_scale = jnp.exp(jax.random.uniform(jax.random.fold_in(key, 21), (TOKENS, 1), jnp.float32, 0.0, math.log(10.0)))
    col_scale = jnp.exp(jax.random.uniform(jax.random.fold_in(key, 22), (1, D), jnp.float32, 0.0, math.log(10.0)))
    base = jax.random.normal(jax.random.fold_in(key, 23), (TOKENS, D), jnp.float32)
    return jnp.clip(base * row_scale * col_scale / 15.0, -8.0, 8.0).astype(jnp.bfloat16)


def block_levels(rng, shape, shards, low, top_value):
    gain = 1.0
    for position, blocks in shards:
        steps = jax.random.uniform(jax.random.fold_in(jax.random.fold_in(rng, 6), position), (blocks,), jnp.float32, low / len(shards), top_value / len(shards))
        gain = gain * jnp.repeat(jnp.exp(steps), shape[position] // blocks).reshape((-1,) + (1,) * (len(shape) - 1 - position))
    return gain


def length_profile(number_of, total, most, lean):
    weights = [(1 << 20) // math.isqrt(standing ** lean) + 1 for standing in range(2, number_of + 1)]
    spare, given = total - most - (number_of - 1), [1] * (number_of - 1)
    while spare > 0:
        free = [i for i in range(number_of - 1) if given[i] < most]
        whole, left = sum([weights[i] for i in free]), spare
        for i in free:
            more = min(most - given[i], max(1, left * weights[i] // whole), spare)
            given[i] = given[i] + more
            spare = spare - more
    return np.array([most] + given)


def ragged(rng, amount, total, reach, slope):
    if amount == 2:
        one = jax.random.randint(rng, (), max(1, total - reach), min(reach, total - 1) + 1)
        return jnp.stack([one, total - one])
    sizes = jnp.asarray(length_profile(amount, total, reach, slope), jnp.int32)
    pairs = (amount - 1) // 2
    source_of, taker = sizes[1:1 + 2 * pairs:2], sizes[2:2 + 2 * pairs:2]
    slack = jnp.minimum(source_of - 1, reach - taker)
    passed = jax.random.randint(jax.random.fold_in(rng, 1), (pairs,), 0, 1 << 20) % (slack + 1)
    sizes = sizes.at[1:1 + 2 * pairs:2].set(source_of - passed).at[2:2 + 2 * pairs:2].set(taker + passed)
    return sizes[jax.random.permutation(jax.random.fold_in(rng, 2), amount)]


def scatter_about(rng, shape, deviation, most, pieces=(), kind=jnp.bfloat16):
    factor_of = block_levels(rng, shape, pieces, -0.22, 0.18) if pieces else 1.0
    entries = jax.random.normal(rng, shape, jnp.float32) * deviation * factor_of
    return jnp.minimum(jnp.maximum(entries, -most), most).astype(kind)


def setup_inputs(seed: int = 0, part: int = 0) -> dict:
    arg_keys = jax.random.split(jax.random.key(seed), 9)
    part_keys = jax.random.split(jax.random.fold_in(arg_keys[8], part), 9)
    return {
        "hidden_in": draw_hidden_in(jax.random.fold_in(jax.random.fold_in(arg_keys[8], part), 71), part),
        "norm_gain": jnp.clip(1.0 + 0.18 * jax.random.normal(arg_keys[1], (D,), jnp.float32), 0.099609375, 1.8984375).astype(jnp.bfloat16),
        "w_query": draw_w_query(jax.random.fold_in(arg_keys[8], 71), part),
        "w_key": draw_w_key(jax.random.fold_in(arg_keys[8], 71), part),
        "w_value": scatter_about(arg_keys[4], (D, HD), D ** -0.5, 0.125, ((0, 32),)),
        "w_out": scatter_about(arg_keys[5], (HEADS * HD, D), (HEADS * HD // 25) ** -0.5, 0.625, ((0, 32),)),
        "seg_ids": jnp.searchsorted(jnp.cumsum(ragged(part_keys[6], SEGS, TOKENS, TOKENS - TOK_DEV, 2)), jnp.arange(TOKENS), side="right").astype(jnp.int32),
        "cache_slot": jax.random.permutation(part_keys[7], BLOCKS).astype(jnp.int32),
    }


EPSILON = 1e-06

def normalize(hidden_in, norm_gain):
    values_wide = hidden_in.astype(jnp.float32)
    mean_square = lax.optimization_barrier(jnp.mean(values_wide * values_wide, axis=1, keepdims=True))
    return (values_wide * lax.rsqrt(mean_square + EPSILON) * norm_gain.astype(jnp.float32)).astype(jnp.bfloat16)

def attend_block(queries, key_rows, value_rows, seg_query, seg_key, pos_query, pos_key):
    row_count = queries.shape[0]
    head_dim = key_rows.shape[1]
    head_count = queries.shape[1] // head_dim
    visible = (seg_query[:, None] == seg_key[None, :]) & (pos_key[None, :] <= pos_query[:, None]) & (pos_key[None, :] > pos_query[:, None] - WINDOW)
    score_scale = 1.0 / head_dim ** 0.5

    def one_head(query_head):
        scores = lax.dot_general(query_head, key_rows, (((1,), (1,)), ((), ())), preferred_element_type=jnp.float32) * score_scale
        scores = jnp.where(visible, scores, -jnp.inf)
        row_top = lax.optimization_barrier(jnp.max(scores, axis=1, keepdims=True))
        weights = jnp.exp(scores - row_top).astype(jnp.bfloat16)
        weight_sum = lax.optimization_barrier(jnp.sum(weights.astype(jnp.float32), axis=1, keepdims=True))
        mixture = jnp.dot(weights, value_rows, preferred_element_type=jnp.float32) / weight_sum
        return mixture.astype(jnp.bfloat16)
    per_head = jnp.transpose(queries.reshape(row_count, head_count, head_dim), (1, 0, 2))
    result = lax.map(one_head, per_head)
    return jnp.transpose(result, (1, 0, 2)).reshape(row_count, head_count * head_dim)

def reference(hidden_in, norm_gain, w_query, w_key, w_value, w_out, seg_ids, cache_slot):
    normed = normalize(hidden_in, norm_gain)
    query = jnp.dot(normed, w_query, preferred_element_type=jnp.float32).astype(jnp.bfloat16)
    key_all = jnp.dot(normed, w_key, preferred_element_type=jnp.float32).astype(jnp.bfloat16)
    value_all = jnp.dot(normed, w_value, preferred_element_type=jnp.float32).astype(jnp.bfloat16)
    token_count = hidden_in.shape[0]
    block_count = token_count // TOK_DEV
    margin = REACH * TOK_DEV
    span = (REACH + 1) * TOK_DEV
    key_pad = jnp.concatenate([jnp.zeros((margin, HD), jnp.bfloat16), key_all], axis=0)
    value_pad = jnp.concatenate([jnp.zeros((margin, HD), jnp.bfloat16), value_all], axis=0)
    seg_whole = seg_ids.astype(jnp.int32)
    seg_pad = jnp.concatenate([jnp.full((margin,), -1, jnp.int32), seg_whole])

    def per_block(block):
        start = (block * TOK_DEV).astype(jnp.int32)
        queries = lax.dynamic_slice_in_dim(query, start, TOK_DEV, 0)
        key_rows = lax.dynamic_slice_in_dim(key_pad, start, span, 0)
        value_rows = lax.dynamic_slice_in_dim(value_pad, start, span, 0)
        seg_query = lax.dynamic_slice_in_dim(seg_whole, start, TOK_DEV, 0)
        seg_key = lax.dynamic_slice_in_dim(seg_pad, start, span, 0)
        pos_query = start + jnp.arange(TOK_DEV, dtype=jnp.int32)
        pos_key = start - margin + jnp.arange(span, dtype=jnp.int32)
        return attend_block(queries, key_rows, value_rows, seg_query, seg_key, pos_query, pos_key)
    attended = lax.map(per_block, jnp.arange(block_count, dtype=jnp.int32)).reshape(token_count, HEADS * HD)
    projected = jnp.dot(attended, w_out, preferred_element_type=jnp.float32)
    hidden_out = (hidden_in.astype(jnp.float32) + projected).astype(jnp.bfloat16)
    stacked = jnp.concatenate([key_all, value_all], axis=1).reshape(token_count // CACHE_BLK, CACHE_BLK, 2 * HD)
    kv_cache = jnp.zeros_like(stacked).at[cache_slot.astype(jnp.int32)].set(stacked).reshape(token_count, 2 * HD)
    return (hidden_out, kv_cache)
```

```python
import jax
import jax.numpy as jnp
from jax import lax
from jax.experimental import pallas as pl
from jax.experimental.pallas import tpu as pltpu
from jax.sharding import Mesh, PartitionSpec as P

WINDOW = 1024
BLK = 128
HD = 128
NY = 4
NX = 4
SEQ = ("y", "x", "core")
EPSILON = 1e-06
LOG2E = 1.4426950408889634
MASKED = -1e30
REL = (0, -1, 1, 2)


def normalize(hidden_in, norm_gain):
    wide = hidden_in.astype(jnp.float32)
    mean_square = jnp.mean(wide * wide, axis=1, keepdims=True)
    return (wide * lax.rsqrt(mean_square + EPSILON) * norm_gain.astype(jnp.float32)).astype(jnp.bfloat16)


def other_core(array):
    return lax.ppermute(array, "core", [(0, 1), (1, 0)])


def turn(array, axis, by):
    n = lax.axis_size(axis)
    return lax.ppermute(array, axis, [(i, (i + by) % n) for i in range(n)])


def hop(array, phase, by):
    pairs = []
    for y in range(NY):
        for x in range(NX):
            for core in range(2):
                along_x = (core == 0) == (phase == 1)
                ty, tx = (y, (x + by) % NX) if along_x else ((y + by) % NY, x)
                pairs.append(((y * NX + x) * 2 + core, (ty * NX + tx) * 2 + core))
    return lax.ppermute(array, SEQ, pairs)


def ring_pieces(array, phase):
    half = array.shape[0] // 2
    before = hop(array, phase, 1)
    after = hop(array, phase, -1)
    far_lo = hop(before[:half], phase, 1)
    far_hi = hop(after[half:], phase, -1)
    return [array, before, after, far_lo, far_hi]


def reorder_kernel(order_ref, src_ref, dst_ref):
    dst_ref[...] = src_ref[...]


def reorder(normed, order):
    rows, cols = normed.shape
    return pl.pallas_call(
        reorder_kernel,
        out_shape=jax.ShapeDtypeStruct(normed.shape, normed.dtype),
        grid_spec=pltpu.PrefetchScalarGridSpec(
            num_scalar_prefetch=1,
            grid=(cols // BLK,),
            in_specs=[pl.BlockSpec((rows, BLK), lambda i, order_ref: (0, order_ref[i]))],
            out_specs=pl.BlockSpec((rows, BLK), lambda i, order_ref: (0, i)),
        ),
        name="reorder",
    )(order, normed)


def project(normed_ref, piece_refs):
    start = 0
    total = None
    for piece_ref in piece_refs:
        depth = piece_ref.shape[0]
        part = jnp.dot(
            normed_ref[:, start : start + depth], piece_ref[...], preferred_element_type=jnp.float32
        )
        total = part if total is None else total + part
        start += depth
    return total


def project_kernel(normed_ref, p0, p1, p2, p3, p4, out_ref):
    out_ref[...] = project(normed_ref, (p0, p1, p2, p3, p4)).astype(jnp.bfloat16)


def project_columns(normed, pieces, width, index):
    rows = normed.shape[0]
    return pl.pallas_call(
        project_kernel,
        out_shape=jax.ShapeDtypeStruct((rows, width), jnp.bfloat16),
        grid=(1,),
        in_specs=[pl.BlockSpec(normed.shape, lambda i: (0, 0))]
        + [pl.BlockSpec((p.shape[0], width), lambda i: (0, index)) for p in pieces],
        out_specs=pl.BlockSpec((rows, width), lambda i: (0, 0)),
        name="project_columns",
    )(normed, *pieces)


def attend_kernel(normed_ref, p0, p1, p2, p3, p4, key_ref, value_ref, segq_ref, segk_ref, out_ref, q_ref, v_ref):
    rows, width = out_ref.shape
    span = WINDOW + BLK
    q_ref[...] = project(normed_ref, (p0, p1, p2, p3, p4)).astype(jnp.bfloat16)
    v_ref[:, :HD] = value_ref[...]
    v_ref[:, HD:] = jnp.ones(value_ref.shape, jnp.bfloat16)
    factor = LOG2E / HD**0.5

    def block(b, carry):
        first = pl.multiple_of(b * BLK, BLK)
        row = lax.broadcasted_iota(jnp.int32, (BLK, span), 0)
        col = lax.broadcasted_iota(jnp.int32, (BLK, span), 1)
        near = (col > row) & (col <= row + WINDOW) & (segq_ref[b] == segk_ref[b])
        bias = jnp.where(near, 0.0, MASKED)
        keys = key_ref[pl.ds(first, span), :]
        values = v_ref[pl.ds(first, span), :]
        for head in range(width // HD):
            query = q_ref[pl.ds(first, BLK), head * HD : (head + 1) * HD]
            scores = lax.dot_general(
                query, keys, (((1,), (1,)), ((), ())), preferred_element_type=jnp.float32
            )
            scores = scores * factor + bias
            top = jnp.max(scores, axis=1, keepdims=True)
            weights = jnp.exp2(scores - top).astype(jnp.bfloat16)
            mixed = jnp.dot(weights, values, preferred_element_type=jnp.float32)
            out_ref[pl.ds(first, BLK), head * HD : (head + 1) * HD] = (
                mixed[:, :HD] / mixed[:, HD:]
            ).astype(jnp.bfloat16)
        return carry

    lax.fori_loop(0, rows // BLK, block, 0)


def attend(normed, pieces, width, index, keys, values, segq, segk):
    rows = normed.shape[0]
    whole = lambda a: pl.BlockSpec(a.shape, lambda i: (0,) * a.ndim)
    return pl.pallas_call(
        attend_kernel,
        out_shape=jax.ShapeDtypeStruct((rows, width), jnp.bfloat16),
        grid=(1,),
        in_specs=[whole(normed)]
        + [pl.BlockSpec((p.shape[0], width), lambda i: (0, index)) for p in pieces]
        + [whole(keys), whole(values), whole(segq), whole(segk)],
        out_specs=pl.BlockSpec((rows, width), lambda i: (0, 0)),
        scratch_shapes=[
            pltpu.VMEM((rows, width), jnp.bfloat16),
            pltpu.VMEM((keys.shape[0], 2 * HD), jnp.bfloat16),
        ],
        name="attend",
    )(normed, *pieces, keys, values, segq, segk)


def pick_kernel(index_ref, a, b, c, d, oa, ob, oc, od):
    oa[...] = a[...]
    ob[...] = b[...]
    oc[...] = c[...]
    od[...] = d[...]


def pick_blocks(blocks, index):
    count = index.shape[1]
    shape = (1,) + blocks.shape[1:]
    spec = lambda k: pl.BlockSpec(shape, lambda i, index_ref: (index_ref[k, i], 0, 0))
    out = pl.BlockSpec(shape, lambda i, index_ref: (i, 0, 0))
    return pl.pallas_call(
        pick_kernel,
        out_shape=[jax.ShapeDtypeStruct((count,) + blocks.shape[1:], blocks.dtype)] * 4,
        grid_spec=pltpu.PrefetchScalarGridSpec(
            num_scalar_prefetch=1,
            grid=(count,),
            in_specs=[spec(k) for k in range(4)],
            out_specs=[out] * 4,
        ),
        name="pick_blocks",
    )(index, blocks, blocks, blocks, blocks)


def place(difference):
    d = difference % 4
    return jnp.where(d == 0, 0, jnp.where(d == 3, 1, jnp.where(d == 1, 2, 3)))


def shards(hidden_in, norm_gain, w_query, w_key, w_value, w_out, seg_ids, cache_slot):
    row_count, width = hidden_in.shape
    half = width // 2
    y, x, core = (lax.axis_index(a) for a in SEQ)
    first_core = core == 0
    chip = y * NX + x

    part0 = jnp.concatenate([w_query[:, :half], w_key], axis=1)
    part1 = jnp.concatenate([w_query[:, half:], w_value], axis=1)
    keep = jnp.where(first_core, part0, part1)
    taken = other_core(jnp.where(first_core, part1, part0))
    own = jnp.concatenate(
        [jnp.where(first_core, keep, taken), jnp.where(first_core, taken, keep)], axis=0
    )
    ring = jnp.concatenate(ring_pieces(own, 1), axis=0)
    pieces = ring_pieces(ring, 2)
    w_out_whole = lax.all_gather(w_out, SEQ, axis=0, tiled=True)

    outer, inner = (jnp.asarray(REL, jnp.int32)[:, None], jnp.asarray(REL, jnp.int32)[None, :])
    order_0 = ((y + outer) % NY) * NX + (x + inner) % NX
    order_1 = ((y + inner) % NY) * NX + (x + outer) % NX
    order = jnp.where(first_core, order_0, order_1).reshape(NY * NX)

    mine = normalize(hidden_in, norm_gain)
    theirs = other_core(mine)
    normed = jnp.concatenate(
        [jnp.where(first_core, mine, theirs), jnp.where(first_core, theirs, mine)], axis=0
    )
    normed = reorder(normed, order)
    chip_rows = 2 * row_count

    made = project_columns(normed, pieces, HD, half // HD)
    seq_count = NY * NX * 2
    back_1 = lax.ppermute(made, SEQ, [(i, i + 2) for i in range(seq_count - 2)])
    short = WINDOW - chip_rows
    back_2 = lax.ppermute(made[chip_rows - short :], SEQ, [(i, i + 4) for i in range(seq_count - 4)])
    window = jnp.concatenate([back_2, back_1, made], axis=0)
    swapped = other_core(window)
    keys = jnp.where(first_core, window, swapped)
    values = jnp.where(first_core, swapped, window)

    seg_pad = jnp.concatenate([jnp.full((WINDOW,), -1, jnp.int32), seg_ids])
    seg_here = lax.dynamic_slice_in_dim(seg_pad, chip * chip_rows, WINDOW + chip_rows, 0)
    blocks = chip_rows // BLK
    segq = seg_here[WINDOW:].reshape(blocks, BLK, 1)
    segk = jnp.stack([seg_here[b * BLK : b * BLK + WINDOW + BLK] for b in range(blocks)])[:, None, :]

    group = 4 * HD
    kept, got = [], []
    for index in range(half // group):
        attended = attend(normed, pieces, group, index, keys, values, segq, segk)
        low, high = attended[:row_count], attended[row_count:]
        kept.append(jnp.where(first_core, low, high))
        got.append(other_core(jnp.where(first_core, high, low)))
    kept = jnp.concatenate(kept, axis=1)
    got = jnp.concatenate(got, axis=1)
    columns = jnp.concatenate(
        [jnp.where(first_core, kept, got), jnp.where(first_core, got, kept)], axis=1
    )
    projected = jnp.dot(columns, w_out_whole, preferred_element_type=jnp.float32)
    hidden_out = (hidden_in.astype(jnp.float32) + projected).astype(jnp.bfloat16)

    made = made.reshape(blocks, BLK, HD)
    column = jnp.concatenate([made, turn(made, "y", 1), turn(made, "y", -1), turn(made, "y", 2)], axis=0)
    total = cache_slot.shape[0]
    ids = jnp.arange(total, dtype=jnp.int32)
    source_of = jnp.sum(jnp.where(cache_slot[None, :] == ids[:, None], ids[None, :], 0), axis=1)
    row_sources = lax.dynamic_slice_in_dim(source_of, y * NX * blocks, NX * blocks, 0).reshape(NX, blocks)
    source_y = row_sources // (NX * blocks)
    source_x = (row_sources // blocks) % NX
    local = place(source_y - y) * blocks + row_sources % blocks
    targets = (x + jnp.asarray((0, 1, -1, 2), jnp.int32)) % NX
    here, right, left, across = pick_blocks(column, jnp.take(local, targets, axis=0))
    arrived = [here, turn(right, "x", 1), turn(left, "x", -1), turn(across, "x", 2)]
    where_from = place(jnp.take(source_x, x, axis=0) - x)[:, None, None]
    owned = arrived[3]
    for k in (2, 1, 0):
        owned = jnp.where(where_from == k, arrived[k], owned)
    low, high = owned[: blocks // 2], owned[blocks // 2 :]
    cache_keep = jnp.where(first_core, low, high)
    cache_got = other_core(jnp.where(first_core, high, low))
    kv_cache = jnp.concatenate(
        [jnp.where(first_core, cache_keep, cache_got), jnp.where(first_core, cache_got, cache_keep)], axis=2
    ).reshape(row_count, 2 * HD)
    return (hidden_out, kv_cache)


def solution(mesh):
    grid = Mesh(mesh.devices.reshape(NY, NX, 2, mesh.devices.shape[1]), SEQ + ("grp",))
    everywhere = P(("grp",) + SEQ, None)
    in_specs = (
        everywhere,
        P(),
        P(SEQ, None),
        P(SEQ, None),
        P(SEQ, None),
        P(SEQ, None),
        P("grp"),
        P("grp"),
    )
    return jax.shard_map(
        shards, mesh=grid, in_specs=in_specs, out_specs=(everywhere, everywhere), check_vma=False
    )
```

```python
import jax
import jax.numpy as jnp
from jax import lax
from jax.experimental import pallas as pl
from jax.experimental.pallas import tpu as pltpu
from jax.sharding import Mesh, PartitionSpec as P

WINDOW = 1024
BLK = 128
HD = 128
NY = 4
NX = 4
SEQ = ("y", "x", "core")
EPSILON = 1e-06
LOG2E = 1.4426950408889634
MASKED = -1e30
REL = (0, -1, 1, 2)


def normalize(hidden_in, norm_gain):
    wide = hidden_in.astype(jnp.float32)
    mean_square = jnp.mean(wide * wide, axis=1, keepdims=True)
    return (wide * lax.rsqrt(mean_square + EPSILON) * norm_gain.astype(jnp.float32)).astype(jnp.bfloat16)


def other_core(array):
    return lax.ppermute(array, "core", [(0, 1), (1, 0)])


def turn(array, axis, by):
    n = lax.axis_size(axis)
    return lax.ppermute(array, axis, [(i, (i + by) % n) for i in range(n)])


def hop(array, phase, by):
    pairs = []
    for y in range(NY):
        for x in range(NX):
            for core in range(2):
                along_x = (core == 0) == (phase == 1)
                ty, tx = (y, (x + by) % NX) if along_x else ((y + by) % NY, x)
                pairs.append(((y * NX + x) * 2 + core, (ty * NX + tx) * 2 + core))
    return lax.ppermute(array, SEQ, pairs)


def ring_pieces(array, phase):
    half = array.shape[0] // 2
    before = hop(array, phase, 1)
    after = hop(array, phase, -1)
    far_lo = hop(before[:half], phase, 1)
    far_hi = hop(after[half:], phase, -1)
    return [array, before, after, far_lo, far_hi]


def place(difference):
    d = lax.rem(difference, 4)
    return jnp.where(d == 0, 0, jnp.where(d == 3, 1, jnp.where(d == 1, 2, 3)))


def block_order(meta_ref):
    y, x, core = meta_ref[0], meta_ref[1], meta_ref[2]
    places = []
    for outer in REL:
        for inner in REL:
            dy = jnp.where(core == 0, outer, inner)
            dx = jnp.where(core == 0, inner, outer)
            places.append(lax.rem(y + dy + NY, NY) * NX + lax.rem(x + dx + NX, NX))
    return places


def assemble(piece_refs, places, weight_ref, shift=0):
    j = 0
    for piece_ref in piece_refs:
        for start in range(0, piece_ref.shape[0], BLK):
            to = lax.rem(places[j] + shift, NY * NX) * BLK
            weight_ref[pl.ds(pl.multiple_of(to, BLK), BLK), :] = piece_ref[start : start + BLK, :]
            j += 1


def kv_kernel(meta_ref, mine_ref, theirs_ref, p0, p1, p2, p3, p4, ring_ref, made_ref, ring_out_ref, w_ref):
    assemble((p0, p1, p2, p3, p4), block_order(meta_ref), w_ref)
    rows = mine_ref.shape[0]
    core = meta_ref[2]
    for ref, at in ((mine_ref, core * rows), (theirs_ref, (1 - core) * rows)):
        made_ref[pl.ds(pl.multiple_of(at, BLK), rows), :] = jnp.dot(
            ref[...], w_ref[...], preferred_element_type=jnp.float32
        ).astype(jnp.bfloat16)


def project_kv(meta, mine, theirs, pieces, index, ring):
    rows, depth = mine.shape
    anywhere = pl.BlockSpec(memory_space=pl.ANY)
    return pl.pallas_call(
        kv_kernel,
        out_shape=[
            jax.ShapeDtypeStruct((2 * rows, HD), jnp.bfloat16),
            jax.ShapeDtypeStruct(ring.shape, ring.dtype),
        ],
        grid_spec=pltpu.PrefetchScalarGridSpec(
            num_scalar_prefetch=1,
            grid=(1,),
            in_specs=[pl.BlockSpec(mine.shape, lambda i, m: (0, 0))] * 2
            + [pl.BlockSpec((p.shape[0], HD), lambda i, m: (0, index)) for p in pieces]
            + [anywhere],
            out_specs=[pl.BlockSpec((2 * rows, HD), lambda i, m: (0, 0)), anywhere],
            scratch_shapes=[pltpu.VMEM((depth, HD), jnp.bfloat16)],
        ),
        input_output_aliases={8: 1},
        name="project_kv",
    )(meta, mine, theirs, *pieces, ring)


def query_kernel(meta_ref, mine_ref, theirs_ref, p0, p1, p2, p3, p4, made_ref, out_ref, made_out_ref, w_ref):
    assemble((p0, p1, p2, p3, p4), block_order(meta_ref), w_ref)
    rows = mine_ref.shape[0]
    factor = LOG2E / HD**0.5
    for ref, at in ((mine_ref, 0), (theirs_ref, rows)):
        out_ref[at : at + rows, :] = (
            jnp.dot(ref[...], w_ref[...], preferred_element_type=jnp.float32) * factor
        ).astype(jnp.bfloat16)


def project_query(meta, mine, theirs, pieces, width, made):
    rows, depth = mine.shape
    group = 4 * HD
    anywhere = pl.BlockSpec(memory_space=pl.ANY)
    return pl.pallas_call(
        query_kernel,
        out_shape=[
            jax.ShapeDtypeStruct((2 * rows, width), jnp.bfloat16),
            jax.ShapeDtypeStruct(made.shape, made.dtype),
        ],
        grid_spec=pltpu.PrefetchScalarGridSpec(
            num_scalar_prefetch=1,
            grid=(width // group,),
            in_specs=[pl.BlockSpec(mine.shape, lambda i, m: (0, 0))] * 2
            + [pl.BlockSpec((p.shape[0], group), lambda i, m: (0, i)) for p in pieces]
            + [anywhere],
            out_specs=[pl.BlockSpec((2 * rows, group), lambda i, m: (0, i)), anywhere],
            scratch_shapes=[pltpu.VMEM((depth, group), jnp.bfloat16)],
        ),
        input_output_aliases={8: 1},
        name="project_query",
    )(meta, mine, theirs, *pieces, made)


def attend_kernel(meta_ref, q_ref, s2, s1, s0, c2, c1, c0, segq_ref, segk_ref, out_ref, key_ref, v_ref):
    rows, width = out_ref.shape
    span = WINDOW + BLK
    core = meta_ref[2]
    blocks = rows // BLK

    def fill(key_refs, value_refs):
        start = 0
        for key, value in zip(key_refs, value_refs):
            count = key.shape[0]
            key_ref[start : start + count, :] = key[...]
            v_ref[start : start + count, :HD] = value[...]
            start += count

    @pl.when(core == 0)
    def _():
        fill((s2, s1, s0), (c2, c1, c0))

    @pl.when(core != 0)
    def _():
        fill((c2, c1, c0), (s2, s1, s0))

    v_ref[:, HD:] = jnp.ones((v_ref.shape[0], HD), jnp.bfloat16)

    def block(b, carry):
        at = lax.rem(b + core * (blocks // 2), blocks)
        first = pl.multiple_of(at * BLK, BLK)
        mine = pl.multiple_of(b * BLK, BLK)
        row = lax.broadcasted_iota(jnp.int32, (BLK, span), 0)
        col = lax.broadcasted_iota(jnp.int32, (BLK, span), 1)
        near = (col > row) & (col <= row + WINDOW) & (segq_ref[at] == segk_ref[at])
        bias = jnp.where(near, 0.0, MASKED)
        keys = key_ref[pl.ds(first, span), :]
        values = v_ref[pl.ds(first, span), :]
        for head in range(width // HD):
            query = q_ref[pl.ds(mine, BLK), head * HD : (head + 1) * HD]
            scores = lax.dot_general(
                query, keys, (((1,), (1,)), ((), ())), preferred_element_type=jnp.float32
            )
            scores = scores + bias
            top = jnp.max(scores, axis=1, keepdims=True)
            weights = jnp.exp2(scores - top).astype(jnp.bfloat16)
            mixed = jnp.dot(weights, values, preferred_element_type=jnp.float32)
            out_ref[pl.ds(mine, BLK), head * HD : (head + 1) * HD] = (
                mixed[:, :HD] / mixed[:, HD:]
            ).astype(jnp.bfloat16)
        return carry

    lax.fori_loop(0, blocks, block, 0)


def attend(meta, query, width, index, same, cross, segq, segk):
    rows = query.shape[0]
    whole = lambda a: pl.BlockSpec(a.shape, lambda i, m: (0,) * a.ndim)
    rest = (*same, *cross, segq, segk)
    return pl.pallas_call(
        attend_kernel,
        out_shape=jax.ShapeDtypeStruct((rows, width), jnp.bfloat16),
        grid_spec=pltpu.PrefetchScalarGridSpec(
            num_scalar_prefetch=1,
            grid=(1,),
            in_specs=[pl.BlockSpec((rows, width), lambda i, m: (0, index))] + [whole(a) for a in rest],
            out_specs=pl.BlockSpec((rows, width), lambda i, m: (0, 0)),
            scratch_shapes=[
                pltpu.VMEM((WINDOW + rows, HD), jnp.bfloat16),
                pltpu.VMEM((WINDOW + rows, 2 * HD), jnp.bfloat16),
            ],
        ),
        name="attend",
    )(meta, query, *rest)


def out_kernel(
    meta_ref, k0, k1, g0, g1, p0, p1, p2, p3, p4, mine_ref, theirs_ref, mine_out, theirs_out, x_ref, w_ref
):
    rows = mine_ref.shape[0]
    group = k0.shape[1]

    @pl.when(pl.program_id(0) == 0)
    def _():
        for n, ref in enumerate((k0, k1)):
            x_ref[:, n * group : (n + 1) * group] = ref[...]
        for n, ref in enumerate((g0, g1)):
            columns = slice((n + 2) * group, (n + 3) * group)
            x_ref[:rows, columns] = ref[rows:, :]
            x_ref[rows:, columns] = ref[:rows, :]

    assemble((p0, p1, p2, p3, p4), block_order(meta_ref), w_ref, meta_ref[2] * (NY * NX // 2))
    for hidden, out, at in ((mine_ref, mine_out, 0), (theirs_ref, theirs_out, rows)):
        product = jnp.dot(x_ref[at : at + rows, :], w_ref[...], preferred_element_type=jnp.float32)
        out[...] = (hidden[...].astype(jnp.float32) + product).astype(jnp.bfloat16)


def project_out(meta, kept, got, pieces, mine, theirs):
    rows, width = mine.shape
    half = width // 2
    step = 256
    whole = lambda a: pl.BlockSpec(a.shape, lambda i, m: (0, 0))
    hidden = pl.BlockSpec((rows, step), lambda i, m: (0, m[2] * (half // step) + i))
    out = pl.BlockSpec((rows, step), lambda i, m: (0, i))
    return pl.pallas_call(
        out_kernel,
        out_shape=[jax.ShapeDtypeStruct((rows, half), jnp.bfloat16)] * 2,
        grid_spec=pltpu.PrefetchScalarGridSpec(
            num_scalar_prefetch=1,
            grid=(half // step,),
            in_specs=[whole(a) for a in (*kept, *got)]
            + [pl.BlockSpec((p.shape[0], step), lambda i, m: (0, i)) for p in pieces]
            + [hidden, hidden],
            out_specs=[out, out],
            scratch_shapes=[
                pltpu.VMEM((2 * rows, width), jnp.bfloat16),
                pltpu.VMEM((width, step), jnp.bfloat16),
            ],
        ),
        name="project_out",
    )(meta, *kept, *got, *pieces, mine, theirs)


def pick_kernel(meta_ref, source_ref, a, b, c, d, after_ref, oa, ob, oc, od):
    oa[...] = a[...]
    ob[...] = b[...]
    oc[...] = c[...]
    od[...] = d[...]


def pick_blocks(meta, source_of, column, per_chip, after):
    shape = (1,) + column.shape[1:]
    row = NX * per_chip

    def spec(target):
        def index(i, m, source_ref):
            y, x = m[0], m[1]
            source = source_ref[y * row + lax.rem(x + target + NX, NX) * per_chip + i]
            return (place(source // row - y + NY) * per_chip + lax.rem(source, per_chip), 0, 0)

        return pl.BlockSpec(shape, index)

    out = pl.BlockSpec(shape, lambda i, m, source_ref: (i, 0, 0))
    return pl.pallas_call(
        pick_kernel,
        out_shape=[jax.ShapeDtypeStruct((per_chip,) + column.shape[1:], column.dtype)] * 4,
        grid_spec=pltpu.PrefetchScalarGridSpec(
            num_scalar_prefetch=2,
            grid=(per_chip,),
            in_specs=[spec(t) for t in (0, 1, -1, 2)] + [pl.BlockSpec(memory_space=pl.ANY)],
            out_specs=[out] * 4,
        ),
        name="pick_blocks",
    )(meta, source_of, column, column, column, column, after)


def own_kernel(meta_ref, source_ref, a, b, c, d, keep_ref, send_ref):
    per_chip = a.shape[0]
    y, x, core = meta_ref[0], meta_ref[1], meta_ref[2]
    refs = (a, b, c, d)
    half = per_chip // 2
    for i in range(half):
        for out_ref, part in ((keep_ref, core), (send_ref, 1 - core)):
            at = part * half + i
            source = source_ref[(y * NX + x) * per_chip + at]
            where = place(lax.rem(source // per_chip, NX) - x + NX)
            for k in range(4):

                @pl.when(where == k)
                def _(out_ref=out_ref, i=i, at=at, k=k):
                    out_ref[i] = refs[k][at]


def own_blocks(meta, source_of, arrived):
    per_chip = arrived[0].shape[0]
    shape = (per_chip // 2,) + arrived[0].shape[1:]
    whole = lambda s: pl.BlockSpec(s, lambda i, m, source_ref: (0, 0, 0))
    return pl.pallas_call(
        own_kernel,
        out_shape=[jax.ShapeDtypeStruct(shape, jnp.bfloat16)] * 2,
        grid_spec=pltpu.PrefetchScalarGridSpec(
            num_scalar_prefetch=2,
            grid=(1,),
            in_specs=[whole(a.shape) for a in arrived],
            out_specs=[whole(shape)] * 2,
        ),
        name="own_blocks",
    )(meta, source_of, *arrived)


def halves(part0, part1, first_core):
    keep = jnp.where(first_core, part0, part1)
    taken = other_core(jnp.where(first_core, part1, part0))
    return jnp.concatenate(
        [jnp.where(first_core, keep, taken), jnp.where(first_core, taken, keep)], axis=0
    )


def send_on(array, chips, cross):
    count = NY * NX
    pairs = [
        (chip * 2 + core, (chip + chips) * 2 + (1 - core if cross else core))
        for chip in range(count - chips)
        for core in range(2)
    ]
    return lax.ppermute(array, SEQ, pairs)


def shards(hidden_in, norm_gain, w_query, w_key, w_value, w_out, seg_ids, cache_slot):
    row_count, width = hidden_in.shape
    half = width // 2
    y, x, core = (lax.axis_index(a) for a in SEQ)
    first_core = core == 0
    chip = y * NX + x
    meta = jnp.stack([y, x, core]).astype(jnp.int32)

    own = halves(
        jnp.concatenate([w_query[:, :half], w_key], axis=1),
        jnp.concatenate([w_query[:, half:], w_value], axis=1),
        first_core,
    )
    own_out = halves(w_out[:, :half], w_out[:, half:], first_core)
    hidden_theirs = other_core(hidden_in)
    ring = jnp.concatenate(ring_pieces(own, 1), axis=0)
    ring_out = jnp.concatenate(ring_pieces(own_out, 1), axis=0)
    pieces = ring_pieces(ring, 2)

    mine = normalize(hidden_in, norm_gain)
    theirs = normalize(hidden_theirs, norm_gain)
    chip_rows = 2 * row_count

    made, ring_out = project_kv(meta, mine, theirs, pieces, half // HD, ring_out)
    short = WINDOW - chip_rows
    tail = made[chip_rows - short :]
    same = (send_on(tail, 2, False), send_on(made, 1, False), made)
    cross = (send_on(tail, 2, True), send_on(made, 1, True), send_on(made, 0, True))
    pieces_out = ring_pieces(ring_out, 2)
    query, made = project_query(meta, mine, theirs, pieces, half, made)

    seg_pad = jnp.concatenate([jnp.full((WINDOW,), -1, jnp.int32), seg_ids])
    seg_here = lax.dynamic_slice_in_dim(seg_pad, chip * chip_rows, WINDOW + chip_rows, 0)
    blocks = chip_rows // BLK
    segq = seg_here[WINDOW:].reshape(blocks, BLK, 1)
    segk = jnp.stack([seg_here[b * BLK : b * BLK + WINDOW + BLK] for b in range(blocks)])[:, None, :]

    group = 4 * HD
    kept = [attend(meta, query, group, i, same, cross, segq, segk) for i in range(half // group)]
    got = [other_core(a) for a in kept]
    out_mine, out_theirs = project_out(meta, kept, got, pieces_out, hidden_in, hidden_theirs)
    out_got = other_core(out_theirs)
    hidden_out = jnp.concatenate(
        [jnp.where(first_core, out_mine, out_got), jnp.where(first_core, out_got, out_mine)], axis=1
    )

    made = made.reshape(blocks, BLK, HD)
    column = jnp.concatenate([made, turn(made, "y", 1), turn(made, "y", -1), turn(made, "y", 2)], axis=0)
    total = cache_slot.shape[0]
    ids = jnp.arange(total, dtype=jnp.int32)
    source_of = jnp.sum(jnp.where(cache_slot[None, :] == ids[:, None], ids[None, :], 0), axis=1)
    here, right, left, across = pick_blocks(meta, source_of, column, blocks, kept[0])
    arrived = (here, turn(right, "x", 1), turn(left, "x", -1), turn(across, "x", 2))
    cache_keep, cache_send = own_blocks(meta, source_of, arrived)
    cache_got = other_core(cache_send)
    kv_cache = jnp.concatenate(
        [jnp.where(first_core, cache_keep, cache_got), jnp.where(first_core, cache_got, cache_keep)], axis=2
    ).reshape(row_count, 2 * HD)
    return (hidden_out, kv_cache)


def solution(mesh):
    grid = Mesh(mesh.devices.reshape(NY, NX, 2, mesh.devices.shape[1]), SEQ + ("grp",))
    everywhere = P(("grp",) + SEQ, None)
    in_specs = (
        everywhere,
        P(),
        P(SEQ, None),
        P(SEQ, None),
        P(SEQ, None),
        P(SEQ, None),
        P("grp"),
        P("grp"),
    )
    return jax.shard_map(
        shards, mesh=grid, in_specs=in_specs, out_specs=(everywhere, everywhere), check_vma=False
    )
```

```python
import jax
import jax.numpy as jnp
from jax import lax
from jax.experimental import pallas as pl
from jax.experimental.pallas import tpu as pltpu
from jax.sharding import Mesh, PartitionSpec as P

WINDOW = 1024
BLK = 128
HD = 128
NY = 4
NX = 4
SEQ = ("y", "x", "core")
EPSILON = 1e-06
LOG2E = 1.4426950408889634
MASKED = -1e30
REL = (0, -1, 1, 2)


def normalize(hidden_in, norm_gain):
    wide = hidden_in.astype(jnp.float32)
    mean_square = jnp.mean(wide * wide, axis=1, keepdims=True)
    return (wide * lax.rsqrt(mean_square + EPSILON) * norm_gain.astype(jnp.float32)).astype(jnp.bfloat16)


def other_core(array):
    return lax.ppermute(array, "core", [(0, 1), (1, 0)])


def turn(array, axis, by):
    n = lax.axis_size(axis)
    return lax.ppermute(array, axis, [(i, (i + by) % n) for i in range(n)])


def hop(array, phase, by):
    pairs = []
    for y in range(NY):
        for x in range(NX):
            for core in range(2):
                along_x = (core == 0) == (phase == 1)
                ty, tx = (y, (x + by) % NX) if along_x else ((y + by) % NY, x)
                pairs.append(((y * NX + x) * 2 + core, (ty * NX + tx) * 2 + core))
    return lax.ppermute(array, SEQ, pairs)


def ring_pieces(array, phase):
    half = array.shape[0] // 2
    before = hop(array, phase, 1)
    after = hop(array, phase, -1)
    far_lo = hop(before[:half], phase, 1)
    far_hi = hop(after[half:], phase, -1)
    return [array, before, after, far_lo, far_hi]


def place(difference):
    d = lax.rem(difference, 4)
    return jnp.where(d == 0, 0, jnp.where(d == 3, 1, jnp.where(d == 1, 2, 3)))


def block_order(meta_ref):
    y, x, core = meta_ref[0], meta_ref[1], meta_ref[2]
    places = []
    for outer in REL:
        for inner in REL:
            dy = jnp.where(core == 0, outer, inner)
            dx = jnp.where(core == 0, inner, outer)
            places.append(lax.rem(y + dy + NY, NY) * NX + lax.rem(x + dx + NX, NX))
    return places


def assemble(piece_refs, places, weight_ref, shift=0):
    j = 0
    for piece_ref in piece_refs:
        for start in range(0, piece_ref.shape[0], BLK):
            to = lax.rem(places[j] + shift, NY * NX) * BLK
            weight_ref[pl.ds(pl.multiple_of(to, BLK), BLK), :] = piece_ref[start : start + BLK, :]
            j += 1


def kv_kernel(meta_ref, mine_ref, theirs_ref, p0, p1, p2, p3, p4, ring_ref, made_ref, ring_out_ref, w_ref):
    assemble((p0, p1, p2, p3, p4), block_order(meta_ref), w_ref)
    rows = mine_ref.shape[0]
    core = meta_ref[2]
    for ref, at in ((mine_ref, core * rows), (theirs_ref, (1 - core) * rows)):
        made_ref[pl.ds(pl.multiple_of(at, BLK), rows), :] = jnp.dot(
            ref[...], w_ref[...], preferred_element_type=jnp.float32
        ).astype(jnp.bfloat16)


def project_kv(meta, mine, theirs, pieces, index, ring):
    rows, depth = mine.shape
    anywhere = pl.BlockSpec(memory_space=pl.ANY)
    return pl.pallas_call(
        kv_kernel,
        out_shape=[
            jax.ShapeDtypeStruct((2 * rows, HD), jnp.bfloat16),
            jax.ShapeDtypeStruct(ring.shape, ring.dtype),
        ],
        grid_spec=pltpu.PrefetchScalarGridSpec(
            num_scalar_prefetch=1,
            grid=(1,),
            in_specs=[pl.BlockSpec(mine.shape, lambda i, m: (0, 0))] * 2
            + [pl.BlockSpec((p.shape[0], HD), lambda i, m: (0, index)) for p in pieces]
            + [anywhere],
            out_specs=[pl.BlockSpec((2 * rows, HD), lambda i, m: (0, 0)), anywhere],
            scratch_shapes=[pltpu.VMEM((depth, HD), jnp.bfloat16)],
        ),
        input_output_aliases={8: 1},
        name="project_kv",
    )(meta, mine, theirs, *pieces, ring)


def query_kernel(meta_ref, mine_ref, theirs_ref, p0, p1, p2, p3, p4, out_ref, w_ref):
    assemble((p0, p1, p2, p3, p4), block_order(meta_ref), w_ref)
    rows = mine_ref.shape[0]
    factor = LOG2E / HD**0.5
    for ref, at in ((mine_ref, 0), (theirs_ref, rows)):
        out_ref[at : at + rows, :] = (
            jnp.dot(ref[...], w_ref[...], preferred_element_type=jnp.float32) * factor
        ).astype(jnp.bfloat16)


def project_query(meta, mine, theirs, pieces, width):
    rows, depth = mine.shape
    group = 4 * HD
    return pl.pallas_call(
        query_kernel,
        out_shape=jax.ShapeDtypeStruct((2 * rows, width), jnp.bfloat16),
        grid_spec=pltpu.PrefetchScalarGridSpec(
            num_scalar_prefetch=1,
            grid=(width // group,),
            in_specs=[pl.BlockSpec(mine.shape, lambda i, m: (0, 0))] * 2
            + [pl.BlockSpec((p.shape[0], group), lambda i, m: (0, i)) for p in pieces],
            out_specs=pl.BlockSpec((2 * rows, group), lambda i, m: (0, i)),
            scratch_shapes=[pltpu.VMEM((depth, group), jnp.bfloat16)],
        ),
        name="project_query",
    )(meta, mine, theirs, *pieces)


def attend_kernel(meta_ref, q_ref, s2, s1, s0, c2, c1, c0, segq_ref, segk_ref, *refs):
    out_ref, key_ref, v_ref = refs[-3:]
    rows, width = out_ref.shape
    span = WINDOW + BLK
    core = meta_ref[2]
    blocks = rows // BLK

    def fill(key_refs, value_refs):
        start = 0
        for key, value in zip(key_refs, value_refs):
            count = key.shape[0]
            key_ref[start : start + count, :] = key[...]
            v_ref[start : start + count, :HD] = value[...]
            start += count

    @pl.when(core == 0)
    def _():
        fill((s2, s1, s0), (c2, c1, c0))

    @pl.when(core != 0)
    def _():
        fill((c2, c1, c0), (s2, s1, s0))

    v_ref[:, HD:] = jnp.ones((v_ref.shape[0], HD), jnp.bfloat16)

    def block(b, carry):
        at = lax.rem(b + core * (blocks // 2), blocks)
        first = pl.multiple_of(at * BLK, BLK)
        mine = pl.multiple_of(b * BLK, BLK)
        row = lax.broadcasted_iota(jnp.int32, (BLK, span), 0)
        col = lax.broadcasted_iota(jnp.int32, (BLK, span), 1)
        near = (col > row) & (col <= row + WINDOW) & (segq_ref[at] == segk_ref[at])
        bias = jnp.where(near, 0.0, MASKED)
        keys = key_ref[pl.ds(first, span), :]
        values = v_ref[pl.ds(first, span), :]
        for head in range(width // HD):
            query = q_ref[pl.ds(mine, BLK), head * HD : (head + 1) * HD]
            scores = lax.dot_general(
                query, keys, (((1,), (1,)), ((), ())), preferred_element_type=jnp.float32
            )
            scores = scores + bias
            top = jnp.max(scores, axis=1, keepdims=True)
            weights = jnp.exp2(scores - top).astype(jnp.bfloat16)
            mixed = jnp.dot(weights, values, preferred_element_type=jnp.float32)
            out_ref[pl.ds(mine, BLK), head * HD : (head + 1) * HD] = (
                mixed[:, :HD] / mixed[:, HD:]
            ).astype(jnp.bfloat16)
        return carry

    lax.fori_loop(0, blocks, block, 0)


def attend(meta, query, width, index, same, cross, segq, segk, after=()):
    rows = query.shape[0]
    tiles = rows * (WINDOW + BLK) * (width // HD)
    whole = lambda a: pl.BlockSpec(a.shape, lambda i, m: (0,) * a.ndim)
    rest = (*same, *cross, segq, segk)
    return pl.pallas_call(
        attend_kernel,
        out_shape=jax.ShapeDtypeStruct((rows, width), jnp.bfloat16),
        grid_spec=pltpu.PrefetchScalarGridSpec(
            num_scalar_prefetch=1,
            grid=(1,),
            in_specs=[pl.BlockSpec((rows, width), lambda i, m: (0, index))] + [whole(a) for a in rest]
            + [pl.BlockSpec(memory_space=pl.ANY)] * len(after),
            out_specs=pl.BlockSpec((rows, width), lambda i, m: (0, 0)),
            scratch_shapes=[
                pltpu.VMEM((WINDOW + rows, HD), jnp.bfloat16),
                pltpu.VMEM((WINDOW + rows, 2 * HD), jnp.bfloat16),
            ],
        ),
        cost_estimate=pl.CostEstimate(
            flops=6 * HD * tiles, transcendentals=tiles, bytes_accessed=4 * rows * width
        ),
        name="attend",
    )(meta, query, *rest, *after)


def out_kernel(
    meta_ref,
    k0,
    k1,
    k2,
    g0,
    g1,
    g2,
    p0,
    p1,
    p2,
    p3,
    p4,
    mine_ref,
    theirs_ref,
    after_ref,
    mine_out,
    theirs_out,
    x_ref,
    w_ref,
):
    rows = mine_ref.shape[0]

    @pl.when(pl.program_id(0) == 0)
    def _():
        start = 0
        for ref in (k0, k1, k2):
            stop = start + ref.shape[1]
            x_ref[:, start:stop] = ref[...]
            start = stop
        for ref in (g0, g1, g2):
            stop = start + ref.shape[1]
            x_ref[:rows, start:stop] = ref[rows:, :]
            x_ref[rows:, start:stop] = ref[:rows, :]
            start = stop

    assemble((p0, p1, p2, p3, p4), block_order(meta_ref), w_ref, meta_ref[2] * (NY * NX // 2))
    for hidden, out, at in ((mine_ref, mine_out, 0), (theirs_ref, theirs_out, rows)):
        product = jnp.dot(x_ref[at : at + rows, :], w_ref[...], preferred_element_type=jnp.float32)
        out[...] = (hidden[...].astype(jnp.float32) + product).astype(jnp.bfloat16)


def project_out(meta, kept, got, pieces, mine, theirs, after):
    rows, width = mine.shape
    half = width // 2
    step = 256
    whole = lambda a: pl.BlockSpec(a.shape, lambda i, m: (0, 0))
    hidden = pl.BlockSpec((rows, step), lambda i, m: (0, m[2] * (half // step) + i))
    out = pl.BlockSpec((rows, step), lambda i, m: (0, i))
    return pl.pallas_call(
        out_kernel,
        out_shape=[jax.ShapeDtypeStruct((rows, half), jnp.bfloat16)] * 2,
        grid_spec=pltpu.PrefetchScalarGridSpec(
            num_scalar_prefetch=1,
            grid=(half // step,),
            in_specs=[whole(a) for a in (*kept, *got)]
            + [pl.BlockSpec((p.shape[0], step), lambda i, m: (0, i)) for p in pieces]
            + [hidden, hidden, pl.BlockSpec(memory_space=pl.ANY)],
            out_specs=[out, out],
            scratch_shapes=[
                pltpu.VMEM((2 * rows, width), jnp.bfloat16),
                pltpu.VMEM((width, step), jnp.bfloat16),
            ],
        ),
        name="project_out",
    )(meta, *kept, *got, *pieces, mine, theirs, after)


def pick_kernel(meta_ref, source_ref, a, b, c, d, after_ref, oa, ob, oc, od):
    oa[...] = a[...]
    ob[...] = b[...]
    oc[...] = c[...]
    od[...] = d[...]


def pick_blocks(meta, source_of, column, per_chip, after):
    shape = (1,) + column.shape[1:]
    row = NX * per_chip

    def spec(target):
        def index(i, m, source_ref):
            y, x = m[0], m[1]
            source = source_ref[y * row + lax.rem(x + target + NX, NX) * per_chip + i]
            return (place(source // row - y + NY) * per_chip + lax.rem(source, per_chip), 0, 0)

        return pl.BlockSpec(shape, index)

    out = pl.BlockSpec(shape, lambda i, m, source_ref: (i, 0, 0))
    return pl.pallas_call(
        pick_kernel,
        out_shape=[jax.ShapeDtypeStruct((per_chip,) + column.shape[1:], column.dtype)] * 4,
        grid_spec=pltpu.PrefetchScalarGridSpec(
            num_scalar_prefetch=2,
            grid=(per_chip,),
            in_specs=[spec(t) for t in (0, 1, -1, 2)] + [pl.BlockSpec(memory_space=pl.ANY)],
            out_specs=[out] * 4,
        ),
        name="pick_blocks",
    )(meta, source_of, column, column, column, column, after)


def own_kernel(meta_ref, source_ref, a, b, c, d, after_ref, keep_ref, send_ref):
    per_chip = a.shape[0]
    y, x, core = meta_ref[0], meta_ref[1], meta_ref[2]
    refs = (a, b, c, d)
    half = per_chip // 2
    for i in range(half):
        for out_ref, part in ((keep_ref, core), (send_ref, 1 - core)):
            at = part * half + i
            source = source_ref[(y * NX + x) * per_chip + at]
            where = place(lax.rem(source // per_chip, NX) - x + NX)
            for k in range(4):

                @pl.when(where == k)
                def _(out_ref=out_ref, i=i, at=at, k=k):
                    out_ref[i] = refs[k][at]


def own_blocks(meta, source_of, arrived, after):
    per_chip = arrived[0].shape[0]
    shape = (per_chip // 2,) + arrived[0].shape[1:]
    whole = lambda s: pl.BlockSpec(s, lambda i, m, source_ref: (0, 0, 0))
    return pl.pallas_call(
        own_kernel,
        out_shape=[jax.ShapeDtypeStruct(shape, jnp.bfloat16)] * 2,
        grid_spec=pltpu.PrefetchScalarGridSpec(
            num_scalar_prefetch=2,
            grid=(1,),
            in_specs=[whole(a.shape) for a in arrived] + [pl.BlockSpec(memory_space=pl.ANY)],
            out_specs=[whole(shape)] * 2,
        ),
        name="own_blocks",
    )(meta, source_of, *arrived, after)


def halves(part0, part1, first_core):
    keep = jnp.where(first_core, part0, part1)
    taken = other_core(jnp.where(first_core, part1, part0))
    return jnp.concatenate(
        [jnp.where(first_core, keep, taken), jnp.where(first_core, taken, keep)], axis=0
    )


def send_on(array, chips, cross):
    count = NY * NX
    pairs = [
        (chip * 2 + core, (chip + chips) * 2 + (1 - core if cross else core))
        for chip in range(count - chips)
        for core in range(2)
    ]
    return lax.ppermute(array, SEQ, pairs)


def shards(hidden_in, norm_gain, w_query, w_key, w_value, w_out, seg_ids, cache_slot):
    row_count, width = hidden_in.shape
    half = width // 2
    y, x, core = (lax.axis_index(a) for a in SEQ)
    first_core = core == 0
    chip = y * NX + x
    meta = jnp.stack([y, x, core]).astype(jnp.int32)

    own = halves(
        jnp.concatenate([w_query[:, :half], w_key], axis=1),
        jnp.concatenate([w_query[:, half:], w_value], axis=1),
        first_core,
    )
    own_out = halves(w_out[:, :half], w_out[:, half:], first_core)
    hidden_theirs = other_core(hidden_in)
    ring = jnp.concatenate(ring_pieces(own, 1), axis=0)
    ring_out = jnp.concatenate(ring_pieces(own_out, 1), axis=0)
    pieces = ring_pieces(ring, 2)

    mine = normalize(hidden_in, norm_gain)
    theirs = normalize(hidden_theirs, norm_gain)
    chip_rows = 2 * row_count

    made, ring_out = project_kv(meta, mine, theirs, pieces, half // HD, ring_out)
    short = WINDOW - chip_rows
    tail = made[chip_rows - short :]
    same = (send_on(tail, 2, False), send_on(made, 1, False), made)
    cross = (send_on(tail, 2, True), send_on(made, 1, True), send_on(made, 0, True))
    pieces_out = ring_pieces(ring_out, 2)
    query = project_query(meta, mine, theirs, pieces, half)

    seg_pad = jnp.concatenate([jnp.full((WINDOW,), -1, jnp.int32), seg_ids])
    seg_here = lax.dynamic_slice_in_dim(seg_pad, chip * chip_rows, WINDOW + chip_rows, 0)
    blocks = chip_rows // BLK
    segq = seg_here[WINDOW:].reshape(blocks, BLK, 1)
    segk = jnp.stack([seg_here[b * BLK : b * BLK + WINDOW + BLK] for b in range(blocks)])[:, None, :]

    made = made.reshape(blocks, BLK, HD)
    column = jnp.concatenate([made, turn(made, "y", 1), turn(made, "y", -1), turn(made, "y", 2)], axis=0)
    total = cache_slot.shape[0]
    ids = jnp.arange(total, dtype=jnp.int32)
    source_of = jnp.sum(jnp.where(cache_slot[None, :] == ids[:, None], ids[None, :], 0), axis=1)

    group = 4 * HD
    first = attend(meta, query, group, 0, same, cross, segq, segk)
    here, right, left, across = pick_blocks(meta, source_of, column, blocks, first)
    second = attend(meta, query, group // 2, 2, same, cross, segq, segk, (here, *pieces_out[1:3]))
    arrived = (here, turn(right, "x", 1), turn(left, "x", -1), turn(across, "x", 2))
    cache_keep, cache_send = own_blocks(meta, source_of, arrived, second)
    cache_got = other_core(cache_send)

    third = attend(meta, query, group // 2, 3, same, cross, segq, segk, (cache_send, *pieces_out[3:]))
    kept = [first, second, third]
    got = [other_core(a) for a in kept]
    out_mine, out_theirs = project_out(
        meta, kept, got, pieces_out, hidden_in, hidden_theirs, cache_send
    )
    out_got = other_core(out_theirs)
    hidden_out = jnp.concatenate(
        [jnp.where(first_core, out_mine, out_got), jnp.where(first_core, out_got, out_mine)], axis=1
    )
    kv_cache = jnp.concatenate(
        [jnp.where(first_core, cache_keep, cache_got), jnp.where(first_core, cache_got, cache_keep)], axis=2
    ).reshape(row_count, 2 * HD)
    return (hidden_out, kv_cache)


def solution(mesh):
    grid = Mesh(mesh.devices.reshape(NY, NX, 2, mesh.devices.shape[1]), SEQ + ("grp",))
    everywhere = P(("grp",) + SEQ, None)
    in_specs = (
        everywhere,
        P(),
        P(SEQ, None),
        P(SEQ, None),
        P(SEQ, None),
        P(SEQ, None),
        P("grp"),
        P("grp"),
    )
    return jax.shard_map(
        shards, mesh=grid, in_specs=in_specs, out_specs=(everywhere, everywhere), check_vma=False
    )
```
